128 devices in a mesh: freq: 8 (over y_hi, z), src: 16 (over y_lo, x, core).
Axes of the slice: x: 4, y: 4 (y_hi: 2, y_lo: 2; y = y_hi * 2 + y_lo), z: 4, core: 2. Of those that a mesh axis runs over, the one named last changes fastest.
Arguments:
- reflection: bfloat16 [2, 128, 2048, 2048], P(None, 'freq', None, 'src'), may hold values from -0.125 to 0.125
- direct_wave: float32 [2048, 128, 128], P('src', 'freq'), may hold values from -6 to 6
- first_arrival: int32 [2048, 64], P(('src', 'freq')), may hold values from 64 to 191
Outputs:
- focus_minus: float32 [2048, 128, 128], P('src', 'freq')
- focus_plus: float32 [2048, 128, 128], P('src', 'freq')
The draws below stay inside these ranges and needn't reach their ends.
All inputs are finite; a program needn't handle non-finite values.
Results may differ from the reference program's by a relative error of at most 0.035.
Values may be sent and summed in bfloat16 or wider, within the bound.
A program may use at most 128 MiB of HBM per device.

```python
import math
import jax
import jax.numpy as jnp
from jax import lax

SRC_DEV = 128
NFOC = 64
NT = 512
ITERS = 2
NFREQ = 128
NX = 2048
N_SRC = 16


def touch_ends(array, key, smallest, largest):
    extent = array.shape
    index_at = [jax.random.randint(jax.random.fold_in(key, axis), (), 0, extent[axis]) for axis in range(len(extent))]
    array = array.at[tuple(index_at)].set(smallest)
    longest = extent.index(max(extent))
    index_at[longest] = (index_at[longest] + 1) % extent[longest]
    return array.at[tuple(index_at)].set(largest)


def raised(entries, rng, source, target, shards_of, factor):
    def block_of(position):
        return (jnp.arange(entries.shape[position]) // (entries.shape[position] // shards_of)).reshape((-1,) + (1,) * (entries.ndim - 1 - position))

    near = jax.random.permutation(rng, shards_of)[block_of(target)]
    other_side = (block_of(target) + shards_of // 2) % shards_of
    return jnp.where((block_of(source) == near) | (block_of(source) == other_side), factor * entries, entries)


def block_scale(stream_key, shape, shards, smallest, high):
    factor_of = 1.0
    for position, blocks in shards:
        heights = jax.random.uniform(jax.random.fold_in(jax.random.fold_in(stream_key, 6), position), (blocks,), jnp.float32, smallest / len(shards), high / len(shards))
        factor_of = factor_of * jnp.repeat(jnp.exp(heights), shape[position] // blocks).reshape((-1,) + (1,) * (len(shape) - 1 - position))
    return factor_of


def bell_draw(stream_key, dims, scale, reach, cuts=(), kind=jnp.bfloat16):
    drawn = scale * jax.random.normal(stream_key, dims, jnp.float32)
    if cuts:
        drawn = drawn * block_scale(stream_key, dims, cuts, -0.22, 0.18)
    return jnp.clip(drawn, -reach, reach).astype(kind)


def gaussian_with(stream_key, shape, scale, most, shards, heavy, kind=jnp.bfloat16):
    array = scale * jax.random.normal(stream_key, shape, jnp.float32)
    if shards:
        array = array * block_scale(stream_key, shape, shards, -0.22, 0.18)
    return jnp.clip(raised(array, jax.random.fold_in(stream_key, 3), *heavy), -most, most).astype(kind)


def setup_inputs(seed: int = 0) -> dict:
    splits = jax.random.split(jax.random.key(seed), 4)
    return {
        "reflection": gaussian_with(splits[0], (2, NFREQ, NX, NX), (2 * NX) ** -0.5, 0.125, ((1, 8), (3, 16)), (3, 2, 16, 2.0)),
        "direct_wave": bell_draw(splits[1], (NX, NFREQ, 2 * NFOC), 1.0, 6.0, ((0, 16), (1, 8)), jnp.float32),
        "first_arrival": touch_ends(jax.random.randint(splits[2], (NX, NFOC), NT // 8, 3 * NT // 8), jax.random.fold_in(splits[2], 1), NT // 8, (3 * NT // 8) - 1).astype(jnp.int32),
    }


def transform_tables(nfreq, ntime):
    freqs = jnp.arange(1, nfreq + 1, dtype=jnp.int32)
    times = jnp.arange(ntime, dtype=jnp.int32)
    phase = ((freqs[:, None] * times[None, :]) % ntime).astype(jnp.float32) * (2.0 * math.pi / ntime)
    cosine = jnp.cos(phase)
    sine = jnp.sin(phase)
    inverse = jnp.stack([cosine * (2.0 / ntime), -sine * (2.0 / ntime)]).astype(jnp.bfloat16)
    forward = jnp.stack([cosine, -sine]).astype(jnp.bfloat16)
    return inverse, forward


def apply_window(spectrum, first_arrival, inverse, forward):
    rows_count, nfreq, width = spectrum.shape
    half = width // 2
    ntime = inverse.shape[2]
    split = spectrum.reshape(rows_count, nfreq, 2, half).astype(jnp.float32)
    signal = jnp.einsum('rfpc,pft->rct', split, inverse.astype(jnp.float32))
    times = jnp.arange(ntime, dtype=jnp.int32)
    limit = first_arrival[:, :, None]
    keep = (times[None, None, :] < limit) | (times[None, None, :] > ntime - limit)
    windowed = jnp.where(keep, signal, jnp.zeros_like(signal)).astype(jnp.bfloat16)
    back = jnp.einsum('rct,pft->rfpc', windowed.astype(jnp.float32), forward.astype(jnp.float32))
    return back.reshape(rows_count, nfreq, width).astype(jnp.float32)


def source_sum(reflection, vectors, factor):
    rounded_all = lax.optimization_barrier(vectors.astype(jnp.bfloat16))

    def one_freq(index):
        slab = lax.dynamic_index_in_dim(reflection, index, 1, keepdims=False)
        column = lax.dynamic_index_in_dim(rounded_all, index, 1, keepdims=False)
        real_rows = slab[0].astype(jnp.float32).reshape(NX, N_SRC, SRC_DEV)
        imag_rows = slab[1].astype(jnp.float32).reshape(NX, N_SRC, SRC_DEV)
        blocks = column.astype(jnp.float32).reshape(N_SRC, SRC_DEV, 2 * NFOC)
        first = jnp.einsum('rds,dsk->drk', real_rows, blocks, precision=lax.Precision.HIGHEST)
        second = jnp.einsum('rds,dsk->drk', imag_rows, blocks, precision=lax.Precision.HIGHEST)
        swapped = jnp.concatenate([-second[..., NFOC:], second[..., :NFOC]], axis=-1)
        terms = lax.optimization_barrier((first + factor * swapped).astype(jnp.bfloat16))
        return jnp.sum(terms.astype(jnp.float32), axis=0).astype(jnp.bfloat16)

    summed = lax.map(one_freq, jnp.arange(NFREQ, dtype=jnp.int32))
    return jnp.transpose(summed, (1, 0, 2))


def reference(reflection, direct_wave, first_arrival):
    inverse, forward = transform_tables(NFREQ, NT)
    focus_plus = direct_wave
    focus_minus = direct_wave
    for iteration in range(ITERS):
        spectrum = source_sum(reflection, focus_plus, 1.0)
        focus_minus = apply_window(spectrum, first_arrival, inverse, forward)
        spectrum = source_sum(reflection, focus_minus, -1.0)
        update = apply_window(spectrum, first_arrival, inverse, forward)
        focus_plus = direct_wave + update
    return focus_minus, focus_plus
```

```python
import functools
import math

import jax
import jax.numpy as jnp
import ml_dtypes
import numpy as np
from jax import lax
from jax.experimental import pallas as pl
from jax.experimental.pallas import tpu as pltpu
from jax.sharding import PartitionSpec as P

NT = 512
ITERS = 2
APPS = 2 * ITERS
NFREQ = 128
PEERS = 8
FDEV = 16
PAIRS = FDEV // 2
BLOCK = 128
C4 = 4
ROWS = 64
CUT = 192
TS = 2 * CUT
TICKS = APPS * 2 * PAIRS
MESH = pl.DeviceIdType.MESH
BF = jnp.bfloat16
F32 = jnp.float32


def tables():
    freqs = np.arange(1, NFREQ + 1, dtype=np.int32)
    times = np.concatenate([np.arange(CUT), np.arange(NT - CUT, NT)]).astype(np.int32)
    phase = ((freqs[:, None] * times[None, :]) % NT).astype(np.float32) * np.float32(2.0 * math.pi / NT)
    cosine, sine = np.cos(phase), np.sin(phase)
    inverse = np.stack([cosine * np.float32(2.0 / NT), -sine * np.float32(2.0 / NT)]).astype(ml_dtypes.bfloat16)
    forward = np.stack([cosine, -sine]).astype(ml_dtypes.bfloat16)
    inv = np.zeros((C4, TS, NFREQ, 2, C4), ml_dtypes.bfloat16)
    fwd = np.zeros((NFREQ, 2, C4, C4, TS), ml_dtypes.bfloat16)
    for c in range(C4):
        inv[c, :, :, :, c] = inverse.transpose(2, 1, 0)
        fwd[:, :, c, c, :] = forward.transpose(1, 0, 2)
    return inv.reshape(C4 * TS, NFREQ * 2 * C4), fwd.reshape(NFREQ * 2 * C4, C4 * TS)


def kernel(r_hbm, dw, fa, inv_hbm, fwd_hbm, out,
           r, inv, fwd, w, p, c_in, t, a_in, b_in, u, y_in, f, g_in, h, v_in, fa_in, wn,
           ss, rs, gss, grs, hss, hrs, fss, frs, lsem, tsem):
    me = lax.axis_index("freq")
    src = lax.axis_index("src")
    core = lax.rem(src, 2)
    x = lax.rem(src // 2, 4)
    y = src // 8

    def at_src(yy, xx, cc):
        return (me, (yy * 4 + xx) * 2 + cc)

    right = lax.rem(x + 1, 4)
    left = lax.rem(x + 3, 4)
    to_core = at_src(y, x, 1 - core)
    to_right = at_src(y, right, core)
    to_left = at_src(y, left, core)
    to_y = at_src(1 - y, x, core)
    peers = [lax.rem(me + i, PEERS) for i in range(1, PEERS)]

    def load_r(k):
        part = pl.ds(2 * k, 2)
        return pltpu.make_async_copy(r_hbm.at[:, part], r.at[:, part], lsem.at[k])

    def load_tables():
        return (pltpu.make_async_copy(inv_hbm, inv, tsem.at[0]), pltpu.make_async_copy(fwd_hbm, fwd, tsem.at[1]))

    for k in range(PAIRS):
        load_r(k).start()
    for copy in load_tables():
        copy.start()

    barrier = pltpu.get_barrier_semaphore()
    for d in [to_core, to_right, to_left, to_y] + [(q, src) for q in peers]:
        pl.semaphore_signal(barrier, inc=1, device_id=d, device_id_type=MESH)
    pl.semaphore_wait(barrier, 4 + PEERS - 1)

    def remote(source, target, send, recv, device):
        return pltpu.make_async_remote_copy(
            src_ref=source, dst_ref=target, send_sem=send, recv_sem=recv, device_id=device, device_id_type=MESH)

    def core_copy(k):
        s = lax.rem(k, 2)
        return remote(p.at[s, 1 - core], c_in.at[s], ss.at[0, s], rs.at[0, s], to_core)

    def a_copies(k):
        s = lax.rem(k, 2)
        return (remote(t.at[s, 2, 0], a_in.at[s, 0], ss.at[1, s], rs.at[1, s], to_right),
                remote(t.at[s, 2, 1], a_in.at[s, 1], ss.at[2, s], rs.at[2, s], to_left))

    def b_copies(k):
        s = lax.rem(k, 2)
        return (remote(t.at[s, 1], b_in.at[s, 0], ss.at[3, s], rs.at[3, s], to_right),
                remote(t.at[s, 3], b_in.at[s, 1], ss.at[4, s], rs.at[4, s], to_left))

    def y_copy(k):
        s = lax.rem(k, 2)
        return remote(u.at[s, 1], y_in.at[s], ss.at[5, s], rs.at[5, s], to_y)

    def fa_copy(i):
        return remote(fa.at[peers[i]], fa_in.at[me], fss.at[i], frs.at[i], (peers[i], src))

    def g_copy(half, i):
        return remote(f.at[half, peers[i]], g_in.at[half, me], gss.at[half, i], grs.at[half, i], (peers[i], src))

    def h_copy(half, i):
        return remote(h.at[half, peers[i]], v_in.at[half, me], hss.at[half, i], hrs.at[half, i], (peers[i], src))

    for i in range(PEERS - 1):
        fa_copy(i).start()
    fa_in[me] = fa[me]

    row = lax.broadcasted_iota(jnp.int32, (PEERS, 2 * C4, BLOCK), 1)

    def stack_rows(half, value, pair, sign):
        for q in range(2):
            part = value[:, 8 * q:8 * q + 8, :]
            turned = jnp.concatenate(
                [jnp.concatenate([part[i, 4:8], part[i, 0:4]], axis=0)[None] for i in range(PEERS)], axis=0)
            turned = jnp.where(row < C4, -sign * turned, sign * turned)
            w[half, 2 * pair + q, :, 0:BLOCK] = part.reshape(ROWS, BLOCK).astype(BF)
            w[half, 2 * pair + q, :, BLOCK:2 * BLOCK] = turned.reshape(ROWS, BLOCK).astype(BF)

    def first_rows(i, _):
        half, pair = i // PAIRS, lax.rem(i, PAIRS)
        stack_rows(half, dw[half, :, pair], pair, 1.0)
        return _

    lax.fori_loop(0, 2 * PAIRS, first_rows, 0)

    def matmul(k):
        s = lax.rem(k, 2)
        pair = lax.rem(k, PAIRS)
        half = lax.rem(k // PAIRS, 2)
        for q in range(2):
            freq = 2 * pair + q
            lhs = w[half, freq]
            for xr in range(4):
                for yr in range(2):
                    yy = y if yr == 0 else 1 - y
                    start = pl.multiple_of((yy * 4 + lax.rem(x + xr, 4)) * 2 * BLOCK, 2 * BLOCK)
                    rows = pl.ds(start, 2 * BLOCK)
                    rhs = jnp.concatenate([r[0, freq, rows, :], r[1, freq, rows, :]], axis=1)
                    term = lax.dot_general(lhs, rhs, (((1,), (1,)), ((), ())), preferred_element_type=F32).astype(BF)
                    p[s, 0, xr, yr, q] = term[:, 0:BLOCK]
                    p[s, 1, xr, yr, q] = term[:, BLOCK:2 * BLOCK]

    def window(n):
        half = lax.rem(n, 2)
        for i in range(PEERS - 1):
            g_copy(half, i).wait()
        spectrum = g_in[half].reshape(NFREQ * 2 * C4, BLOCK)
        time = lax.broadcasted_iota(jnp.int32, (TS, BLOCK), 0)
        time = jnp.where(time < CUT, time, time + (NT - TS)).astype(F32)
        for c in range(C4):
            signal = jnp.dot(inv[c * TS:(c + 1) * TS, :], spectrum, preferred_element_type=F32)
            limit = fa_in[0, pl.ds(half * C4 + c, 1), :]
            for q in range(1, PEERS):
                limit = limit + fa_in[q, pl.ds(half * C4 + c, 1), :]
            keep = (time < limit) | (time > NT - limit)
            wn[c * TS:(c + 1) * TS, :] = jnp.where(keep, signal, 0.0).astype(BF)
        for q in range(PEERS):
            back = jnp.dot(fwd[q * BLOCK:(q + 1) * BLOCK, :], wn[...], preferred_element_type=F32)
            h[half, q] = back.astype(BF).reshape(PAIRS, 16, BLOCK)
        v_in[half, me] = h[half, me]
        for i in range(PEERS - 1):
            h_copy(half, i).start()

    def update(n):
        half = lax.rem(n, 2)
        app = n // 2
        odd = lax.rem(app, 2)
        flag = odd.astype(F32)
        sign = 2.0 * flag - 1.0
        for i in range(PEERS - 1):
            h_copy(half, i).wait()

        def one(pair, _):
            value = v_in[half, :, pair].astype(F32) + flag * dw[half, :, pair]
            out[odd, half, :, pair] = value
            stack_rows(half, value, pair, sign)
            return _

        lax.fori_loop(0, PAIRS, one, 0)

    def tick(k, carry):
        @pl.when((k >= 4) & (k < TICKS + 4))
        def _():
            j = k - 4
            s = lax.rem(j, 2)
            pair = lax.rem(j, PAIRS)
            n = j // PAIRS
            half = lax.rem(n, 2)
            y_copy(j).wait()
            total = u[s, 0].astype(F32) + y_in[s].astype(F32)
            total = total.reshape(2, PEERS, 2 * C4, BLOCK)
            f[half, :, pair] = jnp.concatenate([total[0], total[1]], axis=1).astype(BF)

            @pl.when(pair == PAIRS - 1)
            def _():
                for i in range(PEERS - 1):
                    g_copy(half, i).start()
                g_in[half, me] = f[half, me]

        @pl.when((k >= 3) & (k < TICKS + 3))
        def _():
            j = k - 3
            s = lax.rem(j, 2)
            for copy in b_copies(j):
                copy.wait()
            u[s, 1] = (t[s, 0, 1].astype(F32) + b_in[s, 0, 1].astype(F32) + b_in[s, 1, 1].astype(F32)).astype(BF)
            y_copy(j).start()
            u[s, 0] = (t[s, 0, 0].astype(F32) + b_in[s, 0, 0].astype(F32) + b_in[s, 1, 0].astype(F32)).astype(BF)

        @pl.when((k >= 2) & (k < TICKS + 2))
        def _():
            j = k - 2
            s = lax.rem(j, 2)
            for copy in a_copies(j):
                copy.wait()
            t[s, 1, 0] = (t[s, 1, 0].astype(F32) + a_in[s, 0].astype(F32)).astype(BF)
            t[s, 3, 1] = (t[s, 3, 1].astype(F32) + a_in[s, 1].astype(F32)).astype(BF)
            for copy in b_copies(j):
                copy.start()

        @pl.when((k >= 1) & (k < TICKS + 1))
        def _():
            j = k - 1
            s = lax.rem(j, 2)
            core_copy(j).wait()
            for xr in (2, 1, 3, 0):
                t[s, xr] = (p[s, core, xr].astype(F32) + c_in[s, xr].astype(F32)).astype(BF)
                if xr == 2:
                    for copy in a_copies(j):
                        copy.start()

        @pl.when(k < PAIRS)
        def _():
            load_r(k).wait()

        @pl.when(k < TICKS)
        def _():
            matmul(k)
            core_copy(k).start()

        @pl.when(k == PAIRS)
        def _():
            for copy in load_tables():
                copy.wait()
            for i in range(PEERS - 1):
                fa_copy(i).wait()

        @pl.when((k >= 13) & (lax.rem(k, PAIRS) == 5))
        def _():
            window((k - 13) // PAIRS)

        @pl.when((k >= 15) & (lax.rem(k, PAIRS) == 7))
        def _():
            update((k - 15) // PAIRS)

        return carry

    lax.fori_loop(0, TICKS + PAIRS, tick, 0)


def local(reflection, direct_wave, first_arrival):
    me = lax.axis_index("freq")
    inv, fwd = tables()
    dw = direct_wave.reshape(BLOCK, PAIRS, 2, 2, 2, PEERS, C4)
    dw = dw.transpose(4, 5, 1, 2, 3, 6, 0).reshape(2, PEERS, PAIRS, 16, BLOCK)
    fa = first_arrival.astype(F32).reshape(16, 2, PEERS, C4).transpose(2, 1, 3, 0).reshape(PEERS, 2 * C4, 16)
    fa = jnp.where(jnp.arange(BLOCK) // 16 == me, jnp.tile(fa, (1, 1, PEERS)), 0.0)
    vmem = pl.BlockSpec(memory_space=pltpu.VMEM)
    hbm = pl.BlockSpec(memory_space=pl.ANY)
    dma = pltpu.SemaphoreType.DMA
    unit = (2, ROWS, BLOCK)
    out = pl.pallas_call(
        kernel,
        out_shape=jax.ShapeDtypeStruct((2, 2, PEERS, PAIRS, 16, BLOCK), F32),
        in_specs=[hbm, vmem, vmem, hbm, hbm],
        out_specs=vmem,
        scratch_shapes=[
            pltpu.VMEM(reflection.shape, BF),
            pltpu.VMEM(inv.shape, BF),
            pltpu.VMEM(fwd.shape, BF),
            pltpu.VMEM((2, FDEV, ROWS, 2 * BLOCK), BF),
            pltpu.VMEM((2, 2, 4, 2) + unit, BF),
            pltpu.VMEM((2, 4, 2) + unit, BF),
            pltpu.VMEM((2, 4, 2) + unit, BF),
            pltpu.VMEM((2, 2) + unit, BF),
            pltpu.VMEM((2, 2, 2) + unit, BF),
            pltpu.VMEM((2, 2) + unit, BF),
            pltpu.VMEM((2,) + unit, BF),
            pltpu.VMEM((2, PEERS, PAIRS, 16, BLOCK), BF),
            pltpu.VMEM((2, PEERS, PAIRS, 16, BLOCK), BF),
            pltpu.VMEM((2, PEERS, PAIRS, 16, BLOCK), BF),
            pltpu.VMEM((2, PEERS, PAIRS, 16, BLOCK), BF),
            pltpu.VMEM((PEERS, 2 * C4, BLOCK), F32),
            pltpu.VMEM((C4 * TS, BLOCK), BF),
            dma((6, 2)), dma((6, 2)),
            dma((2, PEERS - 1)), dma((2, PEERS - 1)), dma((2, PEERS - 1)), dma((2, PEERS - 1)),
            dma((PEERS - 1,)), dma((PEERS - 1,)), dma((PAIRS,)), dma((2,)),
        ],
        compiler_params=pltpu.CompilerParams(
            collective_id=0, has_side_effects=True, vmem_limit_bytes=60 << 20),
        name="marchenko",
    )(reflection, dw, fa, jnp.asarray(inv), jnp.asarray(fwd))
    out = out.reshape(2, 2, PEERS, PAIRS, 2, 2, C4, BLOCK).transpose(0, 7, 3, 4, 5, 1, 2, 6)
    out = out.reshape(2, BLOCK, FDEV, 2 * 2 * PEERS * C4)
    return (out[0], out[1])


def solution(mesh):
    in_specs = (P(None, "freq", None, "src"), P("src", "freq", None), P(("src", "freq"), None))
    out_specs = (P("src", "freq", None), P("src", "freq", None))
    return jax.shard_map(local, mesh=mesh, in_specs=in_specs, out_specs=out_specs, check_vma=False)
```

```python
import functools
import math

import jax
import jax.numpy as jnp
import ml_dtypes
import numpy as np
from jax import lax
from jax.experimental import pallas as pl
from jax.experimental.pallas import tpu as pltpu
from jax.sharding import PartitionSpec as P

NT = 512
ITERS = 2
APPS = 2 * ITERS
NFREQ = 128
PEERS = 8
FDEV = 16
PAIRS = FDEV // 2
BLOCK = 128
C4 = 4
ROWS = 64
CUT = 192
TS = 2 * CUT
SLOTS = 16
CSLOTS = 8
D2, D3, D4, D5 = 2, 6, 10, 14
HALF_TICKS = 19
APP_TICKS = 38
WINDOW_AT = 32
UPDATE_AT = 37
MINUS_AT = (APPS - 2) * APP_TICKS + HALF_TICKS + UPDATE_AT + 1
BATCHES = ((0, 6), (6, 2))
MESH = pl.DeviceIdType.MESH
BF = jnp.bfloat16
F32 = jnp.float32


def tables():
    freqs = np.arange(1, NFREQ + 1, dtype=np.int32)
    times = np.concatenate([np.arange(CUT), np.arange(NT - CUT, NT)]).astype(np.int32)
    phase = ((freqs[:, None] * times[None, :]) % NT).astype(np.float32) * np.float32(2.0 * math.pi / NT)
    cosine, sine = np.cos(phase), np.sin(phase)
    inverse = np.stack([cosine * np.float32(2.0 / NT), -sine * np.float32(2.0 / NT)]).astype(ml_dtypes.bfloat16)
    forward = np.stack([cosine, -sine]).astype(ml_dtypes.bfloat16)
    inv = np.zeros((TS, NFREQ, 2, C4), ml_dtypes.bfloat16)
    fwd = np.zeros((NFREQ, 2, C4, TS), ml_dtypes.bfloat16)
    inv[:, :, :, 0] = inverse.transpose(2, 1, 0)
    fwd[:, :, 0, :] = forward.transpose(1, 0, 2)
    return inv.reshape(TS, NFREQ * 2 * C4), fwd.reshape(NFREQ * 2 * C4, TS)


def kernel(r_hbm, wave, fa, inv_hbm, fwd_hbm, minus, plus,
           r, inv, fwd, w, p, c_in, t, a_in, b_in, u, y_in, f, g_in, h, v_in, fa_in, wn, held, dw, out,
           ss, rs, gss, grs, hss, hrs, fss, frs, lsem, tsem):
    me = lax.axis_index("freq")
    src = lax.axis_index("src")
    core = lax.rem(src, 2)
    x = lax.rem(src // 2, 4)
    y = src // 8

    def at_src(yy, xx, cc):
        return (me, (yy * 4 + xx) * 2 + cc)

    right = lax.rem(x + 1, 4)
    left = lax.rem(x + 3, 4)
    to_core = at_src(y, x, 1 - core)
    to_right = at_src(y, right, core)
    to_left = at_src(y, left, core)
    to_y = at_src(1 - y, x, core)
    peers = [lax.rem(me + i, PEERS) for i in range(1, PEERS)]

    def load_r(k):
        part = pl.ds(2 * k, 2)
        return pltpu.make_async_copy(r_hbm.at[:, part], r.at[:, part], lsem.at[k])

    def load_tables():
        return (pltpu.make_async_copy(inv_hbm, inv.at[pl.ds(0, TS)], tsem.at[0]),
                pltpu.make_async_copy(fwd_hbm, fwd.at[:, pl.ds(0, TS)], tsem.at[1]))

    for k in range(PAIRS):
        load_r(k).start()
    for copy in load_tables():
        copy.start()

    barrier = pltpu.get_barrier_semaphore()
    for d in [to_core, to_right, to_left, to_y] + [(q, src) for q in peers]:
        pl.semaphore_signal(barrier, inc=1, device_id=d, device_id_type=MESH)
    pl.semaphore_wait(barrier, 4 + PEERS - 1)

    def remote(source, target, send, recv, device):
        return pltpu.make_async_remote_copy(
            src_ref=source, dst_ref=target, send_sem=send, recv_sem=recv, device_id=device, device_id_type=MESH)

    def core_copy(k):
        s = lax.rem(k, CSLOTS)
        return remote(p.at[s, 1 - core], c_in.at[s], ss.at[0, s], rs.at[0, s], to_core)

    def a_copies(k):
        s = lax.rem(k, SLOTS)
        return (remote(t.at[s, 2, 0], a_in.at[s, 0], ss.at[1, s], rs.at[1, s], to_right),
                remote(t.at[s, 2, 1], a_in.at[s, 1], ss.at[2, s], rs.at[2, s], to_left))

    def b_copies(k):
        s = lax.rem(k, SLOTS)
        return (remote(t.at[s, 1], b_in.at[s, 0], ss.at[3, s], rs.at[3, s], to_right),
                remote(t.at[s, 3], b_in.at[s, 1], ss.at[4, s], rs.at[4, s], to_left))

    def y_copy(k):
        s = lax.rem(k, SLOTS)
        return remote(u.at[s, 1], y_in.at[s], ss.at[5, s], rs.at[5, s], to_y)

    def fa_copy(i):
        return remote(fa.at[peers[i]], fa_in.at[me], fss.at[i], frs.at[i], (peers[i], src))

    def g_copy(half, i, b):
        part = pl.ds(*BATCHES[b])
        return remote(f.at[half, peers[i], part], g_in.at[half, me, part],
                      gss.at[half, b, i], grs.at[half, b, i], (peers[i], src))

    def h_copy(half, i):
        return remote(h.at[half, peers[i]], v_in.at[half, me], hss.at[half, i], hrs.at[half, i], (peers[i], src))

    for i in range(PEERS - 1):
        fa_copy(i).start()
    fa_in[me] = fa[me]

    low = lax.broadcasted_iota(jnp.int32, (PEERS, 2 * C4, BLOCK), 1) < C4

    def expand(c):
        for i in range(NFREQ * 2 * C4 // BLOCK):
            lanes = slice(i * BLOCK, (i + 1) * BLOCK)
            inv[c * TS:(c + 1) * TS, lanes] = pltpu.roll(inv[0:TS, lanes].astype(F32), c, 1).astype(BF)
        for i in range(TS // BLOCK):
            first = fwd[:, i * BLOCK:(i + 1) * BLOCK].astype(F32).reshape(NFREQ, 2 * C4, BLOCK)
            fwd[:, c * TS + i * BLOCK:c * TS + (i + 1) * BLOCK] = pltpu.roll(first, c, 1).reshape(-1, BLOCK).astype(BF)

    def stack_rows(half, part, freq, sign):
        turned = pltpu.roll(part, C4, 1)
        turned = jnp.where(low, -sign * turned, sign * turned)
        w[half, freq, :, 0:BLOCK] = part.reshape(ROWS, BLOCK).astype(BF)
        w[half, freq, :, BLOCK:2 * BLOCK] = turned.reshape(ROWS, BLOCK).astype(BF)

    def first_rows(freq):
        both = jnp.transpose(wave[pl.ds(freq, BLOCK, stride=FDEV), :])
        re = both[0:ROWS].reshape(PEERS, 2 * C4, BLOCK)
        im = both[ROWS:2 * ROWS].reshape(PEERS, 2 * C4, BLOCK)
        for half, part in ((0, jnp.where(low, re, pltpu.roll(im, C4, 1))), (1, jnp.where(low, pltpu.roll(re, C4, 1), im))):
            dw[half, freq] = part
            stack_rows(half, part, freq, 1.0)

    def emit(odd, target, freq):
        first, second = out[odd, 0, freq], out[odd, 1, freq]
        re = jnp.where(low, first, pltpu.roll(second, C4, 1)).reshape(ROWS, BLOCK)
        im = jnp.where(low, pltpu.roll(first, C4, 1), second).reshape(ROWS, BLOCK)
        target[pl.ds(freq, BLOCK, stride=FDEV), :] = jnp.transpose(jnp.concatenate([re, im], axis=0))

    def matmul(k):
        s = lax.rem(k, CSLOTS)
        freq = lax.rem(k, FDEV)
        lhs = w[lax.rem(k // FDEV, 2), freq]
        for xr in range(4):
            for yr in range(2):
                yy = y if yr == 0 else 1 - y
                start = pl.multiple_of((yy * 4 + lax.rem(x + xr, 4)) * 2 * BLOCK, 2 * BLOCK)
                rows = pl.ds(start, 2 * BLOCK)
                rhs = jnp.concatenate([r[0, freq, rows, :], r[1, freq, rows, :]], axis=1)
                term = lax.dot_general(lhs, rhs, (((1,), (1,)), ((), ())), preferred_element_type=F32).astype(BF)
                p[s, 0, xr, yr] = term[:, 0:BLOCK]
                p[s, 1, xr, yr] = term[:, BLOCK:2 * BLOCK]

    def window(n):
        half = lax.rem(n, 2)
        for b in range(len(BATCHES)):
            for i in range(PEERS - 1):
                g_copy(half, i, b).wait()
        spectrum = g_in[half].reshape(NFREQ * 2 * C4, BLOCK)
        time = lax.broadcasted_iota(jnp.int32, (TS, BLOCK), 0)
        time = jnp.where(time < CUT, time, time + (NT - TS)).astype(F32)
        for c in range(C4):
            signal = jnp.dot(inv[c * TS:(c + 1) * TS, :], spectrum, preferred_element_type=F32)
            limit = fa_in[0, pl.ds(half * C4 + c, 1), :]
            for q in range(1, PEERS):
                limit = limit + fa_in[q, pl.ds(half * C4 + c, 1), :]
            keep = (time < limit) | (time > NT - limit)
            wn[c * TS:(c + 1) * TS, :] = jnp.where(keep, signal, 0.0).astype(BF)
        for i, q in enumerate(peers + [me]):
            rows = pl.ds(pl.multiple_of(q * BLOCK, BLOCK), BLOCK)
            back = jnp.dot(fwd[rows, :], wn[...], preferred_element_type=F32)
            back = back.astype(BF).reshape(PAIRS, 16, BLOCK)
            if i < PEERS - 1:
                h[half, q] = back
                h_copy(half, i).start()
            else:
                v_in[half, me] = back

    def update(n):
        half = lax.rem(n, 2)
        app = n // 2
        odd = lax.rem(app, 2)
        flag = odd.astype(F32)
        sign = 2.0 * flag - 1.0
        for i in range(PEERS - 1):
            h_copy(half, i).wait()

        def one(pair, carry):
            both = v_in[half, :, pair].astype(F32)
            for q in range(2):
                freq = 2 * pair + q
                value = both[:, 2 * C4 * q:2 * C4 * (q + 1), :] + flag * dw[half, freq]
                out[odd, half, freq] = value
                stack_rows(half, value, freq, sign)
            return carry

        lax.fori_loop(0, PAIRS, one, 0)

    def chunk(k, delay):
        k = k + APP_TICKS - delay
        app = k // APP_TICKS - 1
        at = lax.rem(k, APP_TICKS)
        half = jnp.where(at >= HALF_TICKS, 1, 0)
        at = at - half * HALF_TICKS
        return (app >= 0) & (app < APPS) & (at < FDEV), (app * 2 + half) * FDEV + at

    def trace(k, delay):
        some, j = chunk(k, delay)
        return some & (lax.rem(j, FDEV) == 0), j // FDEV

    def tick(k, carry):
        some5, j5 = chunk(k, D5)
        some4, j4 = chunk(k, D4)
        some3, j3 = chunk(k, D3)
        some2, j2 = chunk(k, D2)
        some1, j1 = chunk(k, 0)
        some_w, nw = trace(k, WINDOW_AT)
        some_u, nu = trace(k, UPDATE_AT)

        @pl.when(some5)
        def _():
            s = lax.rem(j5, SLOTS)
            freq = lax.rem(j5, FDEV)
            odd, pair = lax.rem(freq, 2), freq // 2
            half = lax.rem(j5 // FDEV, 2)
            y_copy(j5).wait()
            held[odd] = u[s, 0].astype(F32) + y_in[s].astype(F32)

            @pl.when(odd == 1)
            def _():
                total = held[...].reshape(2, PEERS, 2 * C4, BLOCK)
                f[half, :, pair] = jnp.concatenate([total[0], total[1]], axis=1).astype(BF)

            for b, (first, length) in enumerate(BATCHES):
                @pl.when((odd == 1) & (pair == first + length - 1))
                def _():
                    for i in range(PEERS - 1):
                        g_copy(half, i, b).start()
                    part = pl.ds(first, length)
                    g_in[half, me, part] = f[half, me, part]

        @pl.when(some4)
        def _():
            s = lax.rem(j4, SLOTS)
            for copy in b_copies(j4):
                copy.wait()
            u[s, 1] = (t[s, 0, 1].astype(F32) + b_in[s, 0, 1].astype(F32) + b_in[s, 1, 1].astype(F32)).astype(BF)
            y_copy(j4).start()
            u[s, 0] = (t[s, 0, 0].astype(F32) + b_in[s, 0, 0].astype(F32) + b_in[s, 1, 0].astype(F32)).astype(BF)

        @pl.when(some3)
        def _():
            s = lax.rem(j3, SLOTS)
            for copy in a_copies(j3):
                copy.wait()
            t[s, 1, 0] = (t[s, 1, 0].astype(F32) + a_in[s, 0].astype(F32)).astype(BF)
            t[s, 3, 1] = (t[s, 3, 1].astype(F32) + a_in[s, 1].astype(F32)).astype(BF)
            for copy in b_copies(j3):
                copy.start()

        @pl.when(some2)
        def _():
            s = lax.rem(j2, SLOTS)
            cs = lax.rem(j2, CSLOTS)
            core_copy(j2).wait()
            for xr in (2, 1, 3, 0):
                t[s, xr] = (p[cs, core, xr].astype(F32) + c_in[cs, xr].astype(F32)).astype(BF)
                if xr == 2:
                    for copy in a_copies(j2):
                        copy.start()

        @pl.when((k < FDEV) & (lax.rem(k, 2) == 0))
        def _():
            load_r(k // 2).wait()

        @pl.when(k < FDEV)
        def _():
            first_rows(k)

        @pl.when(some1)
        def _():
            matmul(j1)
            core_copy(j1).start()

        @pl.when(k == FDEV)
        def _():
            for copy in load_tables():
                copy.wait()
            for i in range(PEERS - 1):
                fa_copy(i).wait()

        for c in range(1, C4):
            @pl.when(k == FDEV + 2 * c)
            def _():
                expand(c)

        @pl.when(some_w)
        def _():
            window(nw)

        @pl.when(some_u)
        def _():
            update(nu)

        @pl.when((k >= MINUS_AT) & (k < MINUS_AT + FDEV))
        def _():
            emit(0, minus, k - MINUS_AT)

        return carry

    lax.fori_loop(0, (APPS - 1) * APP_TICKS + HALF_TICKS + UPDATE_AT + 1, tick, 0)

    def last(freq, carry):
        emit(1, plus, freq)
        return carry

    lax.fori_loop(0, FDEV, last, 0)


def local(reflection, direct_wave, first_arrival):
    me = lax.axis_index("freq")
    inv, fwd = tables()
    wave = direct_wave.reshape(BLOCK * FDEV, BLOCK)
    fa = first_arrival.astype(F32).reshape(16, PEERS, 2 * C4).transpose(1, 2, 0)
    fa = jnp.where(jnp.arange(BLOCK) // 16 == me, jnp.tile(fa, (1, 1, PEERS)), 0.0)
    vmem = pl.BlockSpec(memory_space=pltpu.VMEM)
    hbm = pl.BlockSpec(memory_space=pl.ANY)
    dma = pltpu.SemaphoreType.DMA
    unit = (ROWS, BLOCK)
    outs = pl.pallas_call(
        kernel,
        out_shape=[jax.ShapeDtypeStruct(wave.shape, F32)] * 2,
        in_specs=[hbm, vmem, vmem, hbm, hbm],
        out_specs=[vmem, vmem],
        scratch_shapes=[
            pltpu.VMEM(reflection.shape, BF),
            pltpu.VMEM((C4 * TS, inv.shape[1]), BF),
            pltpu.VMEM((fwd.shape[0], C4 * TS), BF),
            pltpu.VMEM((2, FDEV, ROWS, 2 * BLOCK), BF),
            pltpu.VMEM((CSLOTS, 2, 4, 2) + unit, BF),
            pltpu.VMEM((CSLOTS, 4, 2) + unit, BF),
            pltpu.VMEM((SLOTS, 4, 2) + unit, BF),
            pltpu.VMEM((SLOTS, 2) + unit, BF),
            pltpu.VMEM((SLOTS, 2, 2) + unit, BF),
            pltpu.VMEM((SLOTS, 2) + unit, BF),
            pltpu.VMEM((SLOTS,) + unit, BF),
            pltpu.VMEM((2, PEERS, PAIRS, 16, BLOCK), BF),
            pltpu.VMEM((2, PEERS, PAIRS, 16, BLOCK), BF),
            pltpu.VMEM((2, PEERS, PAIRS, 16, BLOCK), BF),
            pltpu.VMEM((2, PEERS, PAIRS, 16, BLOCK), BF),
            pltpu.VMEM((PEERS, 2 * C4, BLOCK), F32),
            pltpu.VMEM((C4 * TS, BLOCK), BF),
            pltpu.VMEM((2, ROWS, BLOCK), F32),
            pltpu.VMEM((2, FDEV, PEERS, 2 * C4, BLOCK), F32),
            pltpu.VMEM((2, 2, FDEV, PEERS, 2 * C4, BLOCK), F32),
            dma((6, SLOTS)), dma((6, SLOTS)),
            dma((2, len(BATCHES), PEERS - 1)), dma((2, len(BATCHES), PEERS - 1)),
            dma((2, PEERS - 1)), dma((2, PEERS - 1)),
            dma((PEERS - 1,)), dma((PEERS - 1,)), dma((PAIRS,)), dma((2,)),
        ],
        compiler_params=pltpu.CompilerParams(
            collective_id=0, has_side_effects=True, vmem_limit_bytes=60 << 20),
        name="marchenko",
    )(reflection, wave, fa, jnp.asarray(inv), jnp.asarray(fwd))
    return tuple(o.reshape(direct_wave.shape) for o in outs)


def solution(mesh):
    in_specs = (P(None, "freq", None, "src"), P("src", "freq", None), P(("src", "freq"), None))
    out_specs = (P("src", "freq", None), P("src", "freq", None))
    return jax.shard_map(local, mesh=mesh, in_specs=in_specs, out_specs=out_specs, check_vma=False)
```

```python
import functools
import math

import jax
import jax.numpy as jnp
import ml_dtypes
import numpy as np
from jax import lax
from jax.experimental import pallas as pl
from jax.experimental.pallas import tpu as pltpu
from jax.sharding import PartitionSpec as P

NT = 512
ITERS = 2
APPS = 2 * ITERS
NFREQ = 128
PEERS = 8
FDEV = 16
PAIRS = FDEV // 2
BLOCK = 128
C4 = 4
ROWS = 64
CUT = 192
TS = 2 * CUT
SLOTS = PAIRS
PERIOD = 19
AT_MATMUL = (0, 2, 3, 4, 6, 9, 11, 13)
AT_CORE = (3, 4, 6, 7, 9, 12, 14, 15)
AT_NEAR = (5, 8, 10, 12, 13, 16, 17, 20)
AT_RING = (11, 13, 15, 16, 17, 21, 23, 24)
AT_LAST = (16, 18, 19, 21, 24, 25, 26, 27)
AT_WINDOW = 31
AT_UPDATE = 37
HALVES = 2 * APPS
TICKS = (HALVES - 1) * PERIOD + AT_UPDATE + 1
MINUS_AT = (HALVES - 3) * PERIOD + AT_UPDATE + 1
BATCHES = ((0, 6), (6, 2))
MESH = pl.DeviceIdType.MESH
BF = jnp.bfloat16
F32 = jnp.float32


def tables():
    freqs = np.arange(1, NFREQ + 1, dtype=np.int32)
    times = np.concatenate([np.arange(CUT), np.arange(NT - CUT, NT)]).astype(np.int32)
    phase = ((freqs[:, None] * times[None, :]) % NT).astype(np.float32) * np.float32(2.0 * math.pi / NT)
    cosine, sine = np.cos(phase), np.sin(phase)
    inverse = np.stack([cosine * np.float32(2.0 / NT), -sine * np.float32(2.0 / NT)]).astype(ml_dtypes.bfloat16)
    forward = np.stack([cosine, -sine]).astype(ml_dtypes.bfloat16)
    inv = np.zeros((TS, NFREQ, 2, C4), ml_dtypes.bfloat16)
    fwd = np.zeros((NFREQ, 2, C4, TS), ml_dtypes.bfloat16)
    inv[:, :, :, 0] = inverse.transpose(2, 1, 0)
    fwd[:, :, 0, :] = forward.transpose(1, 0, 2)
    return inv.reshape(TS, NFREQ * 2 * C4), fwd.reshape(NFREQ * 2 * C4, TS)


def kernel(r_hbm, wave, fa, inv_hbm, fwd_hbm, minus, plus,
           r, inv, fwd, w, p, c_in, t, a_in, b_in, u, y_in, f, g_in, h, v_in, fa_in, wn, dw, out,
           ss, rs, gss, grs, hss, hrs, fss, frs, lsem, tsem):
    me = lax.axis_index("freq")
    src = lax.axis_index("src")
    core = lax.rem(src, 2)
    x = lax.rem(src // 2, 4)
    y = src // 8

    def at_src(yy, xx, cc):
        return (me, (yy * 4 + xx) * 2 + cc)

    right = lax.rem(x + 1, 4)
    left = lax.rem(x + 3, 4)
    to_core = at_src(y, x, 1 - core)
    to_right = at_src(y, right, core)
    to_left = at_src(y, left, core)
    to_y = at_src(1 - y, x, core)
    peers = [lax.rem(me + i, PEERS) for i in range(1, PEERS)]

    def load_r(k):
        part = pl.ds(2 * k, 2)
        return pltpu.make_async_copy(r_hbm.at[:, part], r.at[:, part], lsem.at[k])

    def load_tables():
        return (pltpu.make_async_copy(inv_hbm, inv.at[pl.ds(0, TS)], tsem.at[0]),
                pltpu.make_async_copy(fwd_hbm, fwd.at[:, pl.ds(0, TS)], tsem.at[1]))

    for k in range(PAIRS):
        load_r(k).start()
    for copy in load_tables():
        copy.start()

    barrier = pltpu.get_barrier_semaphore()
    for d in [to_core, to_right, to_left, to_y] + [(q, src) for q in peers]:
        pl.semaphore_signal(barrier, inc=1, device_id=d, device_id_type=MESH)
    pl.semaphore_wait(barrier, 4 + PEERS - 1)

    def remote(source, target, send, recv, device):
        return pltpu.make_async_remote_copy(
            src_ref=source, dst_ref=target, send_sem=send, recv_sem=recv, device_id=device, device_id_type=MESH)

    def core_copy(k):
        s = lax.rem(k, SLOTS)
        return remote(p.at[s, 1 - core], c_in.at[s], ss.at[0, s], rs.at[0, s], to_core)

    def a_copies(k):
        s = lax.rem(k, SLOTS)
        return (remote(t.at[s, 2, 0], a_in.at[s, 0], ss.at[1, s], rs.at[1, s], to_right),
                remote(t.at[s, 2, 1], a_in.at[s, 1], ss.at[2, s], rs.at[2, s], to_left))

    def b_copies(k):
        s = lax.rem(k, SLOTS)
        return (remote(t.at[s, 1], b_in.at[s, 0], ss.at[3, s], rs.at[3, s], to_right),
                remote(t.at[s, 3], b_in.at[s, 1], ss.at[4, s], rs.at[4, s], to_left))

    def y_copy(k):
        s = lax.rem(k, SLOTS)
        return remote(u.at[s, 1], y_in.at[s], ss.at[5, s], rs.at[5, s], to_y)

    def fa_copy(i):
        return remote(fa.at[peers[i]], fa_in.at[me], fss.at[i], frs.at[i], (peers[i], src))

    def g_copy(half, i, b):
        part = pl.ds(*BATCHES[b])
        return remote(f.at[half, peers[i], part], g_in.at[half, me, part],
                      gss.at[half, b, i], grs.at[half, b, i], (peers[i], src))

    def h_copy(half, i):
        return remote(h.at[half, peers[i]], v_in.at[half, me], hss.at[half, i], hrs.at[half, i], (peers[i], src))

    for i in range(PEERS - 1):
        fa_copy(i).start()
    fa_in[me] = fa[me]

    low = lax.broadcasted_iota(jnp.int32, (PEERS, 2 * C4, BLOCK), 1) < C4

    def expand(c):
        for i in range(NFREQ * 2 * C4 // BLOCK):
            lanes = slice(i * BLOCK, (i + 1) * BLOCK)
            inv[c * TS:(c + 1) * TS, lanes] = pltpu.roll(inv[0:TS, lanes].astype(F32), c, 1).astype(BF)
        for i in range(TS // BLOCK):
            first = fwd[:, i * BLOCK:(i + 1) * BLOCK].astype(F32).reshape(NFREQ, 2 * C4, BLOCK)
            fwd[:, c * TS + i * BLOCK:c * TS + (i + 1) * BLOCK] = pltpu.roll(first, c, 1).reshape(-1, BLOCK).astype(BF)

    def stack_rows(half, part, freq, sign):
        turned = pltpu.roll(part, C4, 1)
        turned = jnp.where(low, -sign * turned, sign * turned)
        w[half, freq, :, 0:BLOCK] = part.reshape(ROWS, BLOCK).astype(BF)
        w[half, freq, :, BLOCK:2 * BLOCK] = turned.reshape(ROWS, BLOCK).astype(BF)

    def first_rows(freq):
        both = jnp.transpose(wave[pl.ds(freq, BLOCK, stride=FDEV), :])
        re = both[0:ROWS].reshape(PEERS, 2 * C4, BLOCK)
        im = both[ROWS:2 * ROWS].reshape(PEERS, 2 * C4, BLOCK)
        for half, part in ((0, jnp.where(low, re, pltpu.roll(im, C4, 1))), (1, jnp.where(low, pltpu.roll(re, C4, 1), im))):
            dw[half, freq] = part
            stack_rows(half, part, freq, 1.0)

    def emit(odd, target, freq):
        first, second = out[odd, 0, freq], out[odd, 1, freq]
        re = jnp.where(low, first, pltpu.roll(second, C4, 1)).reshape(ROWS, BLOCK)
        im = jnp.where(low, pltpu.roll(first, C4, 1), second).reshape(ROWS, BLOCK)
        target[pl.ds(freq, BLOCK, stride=FDEV), :] = jnp.transpose(jnp.concatenate([re, im], axis=0))

    def matmul(k):
        s = lax.rem(k, SLOTS)
        half = lax.rem(k // PAIRS, 2)
        for q in range(2):
            freq = 2 * s + q
            lhs = w[half, freq]
            for xr in range(4):
                for yr in range(2):
                    yy = y if yr == 0 else 1 - y
                    start = pl.multiple_of((yy * 4 + lax.rem(x + xr, 4)) * 2 * BLOCK, 2 * BLOCK)
                    rows = pl.ds(start, 2 * BLOCK)
                    rhs = jnp.concatenate([r[0, freq, rows, :], r[1, freq, rows, :]], axis=1)
                    term = lax.dot_general(lhs, rhs, (((1,), (1,)), ((), ())), preferred_element_type=F32).astype(BF)
                    p[s, 0, xr, yr, q] = term[:, 0:BLOCK]
                    p[s, 1, xr, yr, q] = term[:, BLOCK:2 * BLOCK]

    def window(n):
        half = lax.rem(n, 2)
        for b in range(len(BATCHES)):
            for i in range(PEERS - 1):
                g_copy(half, i, b).wait()
        spectrum = g_in[half].reshape(NFREQ * 2 * C4, BLOCK)
        time = lax.broadcasted_iota(jnp.int32, (TS, BLOCK), 0)
        time = jnp.where(time < CUT, time, time + (NT - TS)).astype(F32)
        for c in range(C4):
            signal = jnp.dot(inv[c * TS:(c + 1) * TS, :], spectrum, preferred_element_type=F32)
            limit = fa_in[0, pl.ds(half * C4 + c, 1), :]
            for q in range(1, PEERS):
                limit = limit + fa_in[q, pl.ds(half * C4 + c, 1), :]
            keep = (time < limit) | (time > NT - limit)
            wn[c * TS:(c + 1) * TS, :] = jnp.where(keep, signal, 0.0).astype(BF)
        for i, q in enumerate(peers + [me]):
            rows = pl.ds(pl.multiple_of(q * BLOCK, BLOCK), BLOCK)
            back = jnp.dot(fwd[rows, :], wn[...], preferred_element_type=F32)
            back = back.astype(BF).reshape(PAIRS, 16, BLOCK)
            if i < PEERS - 1:
                h[half, q] = back
                h_copy(half, i).start()
            else:
                v_in[half, me] = back

    def update(n):
        half = lax.rem(n, 2)
        app = n // 2
        odd = lax.rem(app, 2)
        flag = odd.astype(F32)
        sign = 2.0 * flag - 1.0
        for i in range(PEERS - 1):
            h_copy(half, i).wait()

        def one(pair, carry):
            both = v_in[half, :, pair].astype(F32)
            for q in range(2):
                freq = 2 * pair + q
                value = both[:, 2 * C4 * q:2 * C4 * (q + 1), :] + flag * dw[half, freq]
                out[odd, half, freq] = value
                stack_rows(half, value, freq, sign)
            return carry

        lax.fori_loop(0, PAIRS, one, 0)

    def chunk(k, at):
        since = k - at[0]
        n = jnp.maximum(since, 0) // PERIOD
        since = since - n * PERIOD
        some, j = since == 0, jnp.int32(0)
        for other in at[1:]:
            some = some | (since == other - at[0])
            j = j + jnp.where(since >= other - at[0], 1, 0)
        return some & (n < HALVES), n * PAIRS + j

    def trace(k, at):
        n = jnp.maximum(k - at, 0) // PERIOD
        return (k - at == n * PERIOD) & (n < HALVES), n

    def tick(k, carry):
        some5, j5 = chunk(k, AT_LAST)
        some4, j4 = chunk(k, AT_RING)
        some3, j3 = chunk(k, AT_NEAR)
        some2, j2 = chunk(k, AT_CORE)
        some1, j1 = chunk(k, AT_MATMUL)
        some_w, nw = trace(k, AT_WINDOW)
        some_u, nu = trace(k, AT_UPDATE)

        @pl.when(some5)
        def _():
            s = lax.rem(j5, SLOTS)
            half = lax.rem(j5 // PAIRS, 2)
            y_copy(j5).wait()
            total = (u[s, 0].astype(F32) + y_in[s].astype(F32)).reshape(2, PEERS, 2 * C4, BLOCK)
            f[half, :, s] = jnp.concatenate([total[0], total[1]], axis=1).astype(BF)
            for b, (first, length) in enumerate(BATCHES):
                @pl.when(s == first + length - 1)
                def _():
                    for i in range(PEERS - 1):
                        g_copy(half, i, b).start()
                    part = pl.ds(first, length)
                    g_in[half, me, part] = f[half, me, part]

        @pl.when(some4)
        def _():
            s = lax.rem(j4, SLOTS)
            for copy in b_copies(j4):
                copy.wait()
            u[s, 1] = (t[s, 0, 1].astype(F32) + b_in[s, 0, 1].astype(F32) + b_in[s, 1, 1].astype(F32)).astype(BF)
            y_copy(j4).start()
            u[s, 0] = (t[s, 0, 0].astype(F32) + b_in[s, 0, 0].astype(F32) + b_in[s, 1, 0].astype(F32)).astype(BF)

        @pl.when(some3)
        def _():
            s = lax.rem(j3, SLOTS)
            for copy in a_copies(j3):
                copy.wait()
            t[s, 1, 0] = (t[s, 1, 0].astype(F32) + a_in[s, 0].astype(F32)).astype(BF)
            t[s, 3, 1] = (t[s, 3, 1].astype(F32) + a_in[s, 1].astype(F32)).astype(BF)
            for copy in b_copies(j3):
                copy.start()

        @pl.when(some2)
        def _():
            s = lax.rem(j2, SLOTS)
            core_copy(j2).wait()
            for xr in (2, 1, 3, 0):
                t[s, xr] = (p[s, core, xr].astype(F32) + c_in[s, xr].astype(F32)).astype(BF)
                if xr == 2:
                    for copy in a_copies(j2):
                        copy.start()

        @pl.when(some1 & (j1 < PAIRS))
        def _():
            load_r(j1).wait()
            for q in range(2):
                first_rows(2 * j1 + q)

        @pl.when(some1)
        def _():
            matmul(j1)
            core_copy(j1).start()

        @pl.when(k == FDEV)
        def _():
            for copy in load_tables():
                copy.wait()
            for i in range(PEERS - 1):
                fa_copy(i).wait()

        for c in range(1, C4):
            @pl.when(k == FDEV + 2 * c)
            def _():
                expand(c)

        @pl.when(some_w)
        def _():
            window(nw)

        @pl.when(some_u)
        def _():
            update(nu)

        @pl.when((k >= MINUS_AT) & (k < MINUS_AT + FDEV))
        def _():
            emit(0, minus, k - MINUS_AT)

        return carry

    lax.fori_loop(0, TICKS, tick, 0)

    def last(freq, carry):
        emit(1, plus, freq)
        return carry

    lax.fori_loop(0, FDEV, last, 0)


def local(reflection, direct_wave, first_arrival):
    me = lax.axis_index("freq")
    inv, fwd = tables()
    wave = direct_wave.reshape(BLOCK * FDEV, BLOCK)
    fa = first_arrival.astype(F32).reshape(16, PEERS, 2 * C4).transpose(1, 2, 0)
    fa = jnp.where(jnp.arange(BLOCK) // 16 == me, jnp.tile(fa, (1, 1, PEERS)), 0.0)
    vmem = pl.BlockSpec(memory_space=pltpu.VMEM)
    hbm = pl.BlockSpec(memory_space=pl.ANY)
    dma = pltpu.SemaphoreType.DMA
    unit = (2, ROWS, BLOCK)
    outs = pl.pallas_call(
        kernel,
        out_shape=[jax.ShapeDtypeStruct(wave.shape, F32)] * 2,
        in_specs=[hbm, vmem, vmem, hbm, hbm],
        out_specs=[vmem, vmem],
        scratch_shapes=[
            pltpu.VMEM(reflection.shape, BF),
            pltpu.VMEM((C4 * TS, inv.shape[1]), BF),
            pltpu.VMEM((fwd.shape[0], C4 * TS), BF),
            pltpu.VMEM((2, FDEV, ROWS, 2 * BLOCK), BF),
            pltpu.VMEM((SLOTS, 2, 4, 2) + unit, BF),
            pltpu.VMEM((SLOTS, 4, 2) + unit, BF),
            pltpu.VMEM((SLOTS, 4, 2) + unit, BF),
            pltpu.VMEM((SLOTS, 2) + unit, BF),
            pltpu.VMEM((SLOTS, 2, 2) + unit, BF),
            pltpu.VMEM((SLOTS, 2) + unit, BF),
            pltpu.VMEM((SLOTS,) + unit, BF),
            pltpu.VMEM((2, PEERS, PAIRS, 16, BLOCK), BF),
            pltpu.VMEM((2, PEERS, PAIRS, 16, BLOCK), BF),
            pltpu.VMEM((2, PEERS, PAIRS, 16, BLOCK), BF),
            pltpu.VMEM((2, PEERS, PAIRS, 16, BLOCK), BF),
            pltpu.VMEM((PEERS, 2 * C4, BLOCK), F32),
            pltpu.VMEM((C4 * TS, BLOCK), BF),
            pltpu.VMEM((2, FDEV, PEERS, 2 * C4, BLOCK), F32),
            pltpu.VMEM((2, 2, FDEV, PEERS, 2 * C4, BLOCK), F32),
            dma((6, SLOTS)), dma((6, SLOTS)),
            dma((2, len(BATCHES), PEERS - 1)), dma((2, len(BATCHES), PEERS - 1)),
            dma((2, PEERS - 1)), dma((2, PEERS - 1)),
            dma((PEERS - 1,)), dma((PEERS - 1,)), dma((PAIRS,)), dma((2,)),
        ],
        compiler_params=pltpu.CompilerParams(
            collective_id=0, has_side_effects=True, vmem_limit_bytes=60 << 20),
        name="marchenko",
    )(reflection, wave, fa, jnp.asarray(inv), jnp.asarray(fwd))
    return tuple(o.reshape(direct_wave.shape) for o in outs)


def solution(mesh):
    in_specs = (P(None, "freq", None, "src"), P("src", "freq", None), P(("src", "freq"), None))
    out_specs = (P("src", "freq", None), P("src", "freq", None))
    return jax.shard_map(local, mesh=mesh, in_specs=in_specs, out_specs=out_specs, check_vma=False)
```
